32 devices in a mesh: facet: 2 (over y), sub: 16 (over z, x, core).
Axes of the slice: x: 2, y: 2, z: 4, core: 2. Of those that a mesh axis runs over, the one named last changes fastest.
Arguments:
- contributions: bfloat16 [16, 16, 2, 2, 192, 192], P('facet', 'sub'), may hold values from -6 to 6
- slot_subgrid: int32 [16, 2, 2], P('sub'), may hold values from -1 to 1, as said below
- vis_count: int32 [2, 16, 2], P('facet', 'sub'), may hold values from 0 to 384, as said below
- vis_uv: float32 [2, 16, 2, 2, 384], P('facet', 'sub'), may hold values from 0 to 512
- vis_obs: float32 [2, 16, 2, 2, 384], P('facet', 'sub'), may hold values from -6 to 6
- vis_weight: float32 [2, 16, 2, 384], P('facet', 'sub'), may hold values from 0.25 to 2
- subgrid_offset: int32 [16, 2, 2], P('sub'), may hold values from 0 to 511
Outputs:
- facet_residual: float32 [16, 2, 512, 512], P('facet', None, 'sub')
The draws below stay inside these ranges and needn't reach their ends.
Inputs may be any that keep to these rules, and one draw needn't show every extreme that they name: `slot_subgrid`: in every column each of the 2 subgrids sits in exactly one of the 2 x 2 slots and the other slots hold -1; in every column the 2 slots of some device are all used. `vis_count`: 0 exactly for slots that hold no subgrid, from 384 // 4 to 384 for the others, and 384 in some slot of every column.
All inputs are finite; a program needn't handle non-finite values.
Results may differ from the reference program's by a relative error of at most 0.013.
Values may be sent and summed in bfloat16 or wider, within the bound.
A program may use at most 128 MiB of HBM per device.

```python
import math
import jax
import jax.numpy as jnp
from jax import lax

SUBGRID = 512
CONTRIB = 192
FACET_SIDE = 4
WIN = 512
VCAP = 384
FACETS = 16
GROUPS = 2
COLUMNS = 16
SG_COL = 2
SLOTS = 2


def slot_layout(key):
    base_key = jax.random.fold_in(key, 7)
    column_keys = jax.random.split(base_key, COLUMNS)

    def one_column(column_key):
        key_group, key_order, key_ids, key_lengths = jax.random.split(column_key, 4)
        capacity = GROUPS * SLOTS
        full_group = jax.random.randint(key_group, (), 0, GROUPS)
        scores = jax.random.permutation(key_order, capacity).astype(jnp.int32)
        owner = jnp.arange(capacity) // SLOTS
        ranked = jnp.where(owner == full_group, scores - capacity, scores)
        ranking = jnp.argsort(ranked, stable=True)
        subgrid_ids = jax.random.permutation(key_ids, SG_COL).astype(jnp.int32)
        slot_table = jnp.full((capacity,), -1, jnp.int32).at[ranking[:SG_COL]].set(subgrid_ids)
        lengths = jax.random.randint(key_lengths, (capacity,), VCAP // 4, VCAP + 1).astype(jnp.int32)
        lengths = lengths.at[ranking[0]].set(VCAP)
        lengths = jnp.where(slot_table >= 0, lengths, 0).astype(jnp.int32)
        return (slot_table.reshape(GROUPS, SLOTS), lengths.reshape(GROUPS, SLOTS))
    return jax.vmap(one_column)(column_keys)


def draw_slot_subgrid(key, part):
    return slot_layout(key)[0]


def draw_vis_count(key, part):
    return jnp.transpose(slot_layout(key)[1], (1, 0, 2))


def plant(drawn, key, least, top_value):
    longest = drawn.shape.index(max(drawn.shape))
    spots = []
    for shift in (0, 1):
        where = [jax.random.randint(jax.random.fold_in(key, axis), (), 0, length) for axis, length in enumerate(drawn.shape)]
        where[longest] = (where[longest] + shift) % drawn.shape[longest]
        spots.append(tuple(where))
    return drawn.at[spots[0]].set(least).at[spots[1]].set(top_value)


def levels(stream_key, extent, cuts, smallest, top_value):
    level, own = 1.0, jax.random.fold_in(stream_key, 6)
    for dim, shards_of in cuts:
        steps = jnp.exp(jax.random.uniform(jax.random.fold_in(own, dim), (shards_of,), jnp.float32, smallest / len(cuts), top_value / len(cuts)))
        level = level * jnp.repeat(steps, extent[dim] // shards_of).reshape([-1 if axis == dim else 1 for axis in range(len(extent))])
    return level


def normal_values(key, extent, scale, reach, cuts=(), kind=jnp.bfloat16):
    drawn = jax.random.normal(key, extent, jnp.float32) * scale
    if len(cuts) > 0:
        drawn = levels(key, extent, cuts, -0.22, 0.18) * drawn
    return jnp.clip(drawn, min=-reach, max=reach).astype(kind)


def setup_inputs(seed: int = 0) -> dict:
    splits = jax.random.split(jax.random.key(seed), 8)
    contributions = normal_values(splits[0], (FACETS, COLUMNS, SG_COL, 2, CONTRIB, CONTRIB), 1.0, 6.0, ((0, 2), (1, 16)))
    slot_subgrid = draw_slot_subgrid(jax.random.fold_in(splits[7], 71), 0)
    vis_count = draw_vis_count(jax.random.fold_in(splits[7], 71), 0)
    vis_uv = jnp.clip(512.0 * jax.random.uniform(splits[3], (GROUPS, COLUMNS, SLOTS, 2, VCAP), jnp.float32) ** levels(splits[3], (GROUPS, COLUMNS, SLOTS, 2, VCAP), ((0, 2), (1, 16)), -0.2, 0.2), 0.0, 512.0)
    vis_obs = normal_values(splits[4], (GROUPS, COLUMNS, SLOTS, 2, VCAP), 1.0, 6.0, ((0, 2), (1, 16)), jnp.float32)
    vis_weight = jnp.clip(jnp.exp(math.log(2.0) - 2.0794415 * jax.random.uniform(splits[5], (GROUPS, COLUMNS, SLOTS, VCAP), jnp.float32) ** levels(splits[5], (GROUPS, COLUMNS, SLOTS, VCAP), ((0, 2), (1, 16)), -0.2, 0.2)), 0.25, 2.0)
    subgrid_offset = plant(jax.random.randint(splits[6], (COLUMNS, SG_COL, 2), 0, WIN), jax.random.fold_in(splits[6], 1), 0, WIN - 1).astype(jnp.int32)
    return dict(contributions=contributions, slot_subgrid=slot_subgrid, vis_count=vis_count, vis_uv=vis_uv, vis_obs=vis_obs, vis_weight=vis_weight, subgrid_offset=subgrid_offset)


def corner_cells(facet_index):
    stride = (SUBGRID - CONTRIB) // (FACET_SIDE - 1)
    return (facet_index // FACET_SIDE * stride, facet_index % FACET_SIDE * stride)

def assemble(blocks):
    subgrid_image = None
    for facet_index in range(FACETS):
        start_row, start_column = corner_cells(facet_index)
        padded = jnp.pad(blocks[facet_index].astype(jnp.float32), ((0, 0), (start_row, SUBGRID - start_row - CONTRIB), (start_column, SUBGRID - start_column - CONTRIB)))
        subgrid_image = padded if subgrid_image is None else subgrid_image + padded
    return subgrid_image.astype(jnp.bfloat16)

def phase_tables(coordinate):
    cell_grid = jnp.arange(SUBGRID, dtype=jnp.float32)
    phase_angle = 2.0 * math.pi / SUBGRID * cell_grid[:, None] * coordinate[None, :]
    return (jnp.cos(phase_angle).astype(jnp.bfloat16), (-jnp.sin(phase_angle)).astype(jnp.bfloat16))

def visit_subgrid(subgrid_image, coordinates, observed, weight, visible_count):
    first_real, first_imaginary = phase_tables(coordinates[0])
    second_real, second_imaginary = phase_tables(coordinates[1])
    cells = SUBGRID
    visits = coordinates.shape[1]
    stacked = jnp.concatenate([subgrid_image[0], subgrid_image[1]], axis=0)
    partial_sums = jnp.dot(stacked, jnp.concatenate([second_real, second_imaginary], axis=1), preferred_element_type=jnp.float32)
    inner_real = partial_sums[:cells, :visits] - partial_sums[cells:, visits:]
    inner_imaginary = partial_sums[:cells, visits:] + partial_sums[cells:, :visits]
    first_rf = first_real.astype(jnp.float32)
    first_if = first_imaginary.astype(jnp.float32)
    model_real = lax.optimization_barrier(jnp.sum(first_rf * inner_real - first_if * inner_imaginary, axis=0)) / SUBGRID
    model_imaginary = lax.optimization_barrier(jnp.sum(first_rf * inner_imaginary + first_if * inner_real, axis=0)) / SUBGRID
    active = jnp.arange(visits) < visible_count
    residual_real = jnp.where(active, weight * (observed[0] - model_real), 0.0).astype(jnp.bfloat16)
    residual_imaginary = jnp.where(active, weight * (observed[1] - model_imaginary), 0.0).astype(jnp.bfloat16)
    real_float = residual_real.astype(jnp.float32)
    imaginary_float = residual_imaginary.astype(jnp.float32)
    lift_real = (first_rf * real_float + first_if * imaginary_float).astype(jnp.bfloat16)
    lift_imaginary = (first_rf * imaginary_float - first_if * real_float).astype(jnp.bfloat16)
    lifted = jnp.concatenate([lift_real, lift_imaginary], axis=0)
    tables = jnp.concatenate([second_real, second_imaginary], axis=0)
    gridded = lax.dot_general(lifted, tables, (((1,), (1,)), ((), ())), preferred_element_type=jnp.float32)
    grid_scale = 1.0 / math.sqrt(VCAP)
    grid_real = (gridded[:cells, :cells] + gridded[cells:, cells:]) * grid_scale
    grid_imaginary = (gridded[cells:, :cells] - gridded[:cells, cells:]) * grid_scale
    grid_both = jnp.stack([grid_real, grid_imaginary])
    pieces = []
    for facet_index in range(FACETS):
        start_row, start_column = corner_cells(facet_index)
        pieces.append(grid_both[:, start_row:start_row + CONTRIB, start_column:start_column + CONTRIB])
    return jnp.stack(pieces).astype(jnp.bfloat16)

def place_piece(accum, pieces, offset):
    anchor = jnp.zeros((), jnp.int32)
    corner_start = (anchor, anchor, offset[0].astype(jnp.int32), offset[1].astype(jnp.int32))
    current = lax.dynamic_slice(accum, corner_start, pieces.shape)
    return lax.dynamic_update_slice(accum, current + pieces.astype(jnp.float32), corner_start)

def fold_edges(accum):
    upper = accum[:, :, :WIN].at[:, :, :CONTRIB].add(accum[:, :, WIN:])
    return upper[..., :WIN].at[..., :CONTRIB].add(upper[..., WIN:])

def reference(contributions, slot_subgrid, vis_count, vis_uv, vis_obs, vis_weight, subgrid_offset):
    padded_width = WIN + CONTRIB
    start_accum = jnp.zeros((FACETS, 2, padded_width, padded_width), jnp.float32)

    def visit_one(position_index, accum):
        column = position_index // SG_COL
        member = position_index % SG_COL
        flattened = slot_subgrid[column].reshape(-1)
        where_slot = jnp.argmax(flattened == member).astype(jnp.int32)
        group_index = where_slot // SLOTS
        slot_index = where_slot % SLOTS
        subgrid_image = assemble(contributions[:, column, member])
        returned = visit_subgrid(subgrid_image, vis_uv[group_index, column, slot_index], vis_obs[group_index, column, slot_index], vis_weight[group_index, column, slot_index], vis_count[group_index, column, slot_index])
        return place_piece(accum, returned, subgrid_offset[column, member])
    accum = lax.fori_loop(0, COLUMNS * SG_COL, visit_one, start_accum)
    window_gain = WIN / (CONTRIB * math.sqrt(SG_COL * COLUMNS))
    return fold_edges(accum) * window_gain
```

```python
import functools
import math

import jax
import jax.numpy as jnp
from jax import lax
from jax.experimental import pallas as pl
from jax.experimental.pallas import tpu as pltpu
from jax.sharding import PartitionSpec as P

SUBGRID = 512
FACET_SIDE = 4
WIN = 512
BLOCK = 16
ALIGNED = 256


def cis(turn):
    turn = turn - jnp.floor(turn + 0.5)
    x = turn * math.pi
    q = x * x
    s = -1.0 / math.factorial(11)
    for order in (9, 7, 5, 3, 1):
        sign = 1.0 if order % 4 == 1 else -1.0
        s = s * q + sign / math.factorial(order)
    s = s * x
    c = 1.0 / math.factorial(12)
    for order in (10, 8, 6, 4, 2, 0):
        sign = 1.0 if order % 4 == 0 else -1.0
        c = c * q + sign / math.factorial(order)
    return 1.0 - 2.0 * s * s, 2.0 * s * c


def turns(k, w):
    high = jnp.floor(w * 4096.0) * (1.0 / 4096.0)
    low = w - high
    p = k * high
    return (p - jnp.floor(p + 0.5)) + k * low


def cmul(a, b):
    return a[0] * b[0] - a[1] * b[1], a[0] * b[1] + a[1] * b[0]


def row_iota(rows, lanes):
    return lax.broadcasted_iota(jnp.int32, (rows, lanes), 0)


def corner(index, stride):
    return lax.div(index, FACET_SIDE) * stride, lax.rem(index, FACET_SIDE) * stride


def partial_models(facet_here, per_group, c_ref, u_of, v_of, put, cs, rhs):
    side = c_ref.shape[-1]
    members = c_ref.shape[1]
    stride = (SUBGRID - side) // (FACET_SIDE - 1)
    across = min(per_group, FACET_SIDE)
    down = per_group // across
    lanes = rhs.shape[1] // 2
    first_row, first_col = corner(facet_here * per_group, stride)
    lines = row_iota(BLOCK, lanes)
    cs[...] = jnp.zeros_like(cs)
    rhs[...] = jnp.zeros_like(rhs)

    @pl.loop(0, members)
    def _(j):
        wu = u_of(j) * (1.0 / SUBGRID)
        wv = v_of(j) * (1.0 / SUBGRID)
        step_v = tuple(jnp.broadcast_to(t, (BLOCK, lanes)) for t in cis(turns(float(BLOCK), wv)))
        step_u = tuple(jnp.broadcast_to(t, (BLOCK, lanes)) for t in cis(turns(float(BLOCK), wu)))
        for b in range(across):
            k = (lines + (first_col + b * stride)).astype(jnp.float32)
            now = cis(turns(k, wv))
            for h in range(side // BLOCK):
                at = b * ALIGNED + h * BLOCK
                rhs[at : at + BLOCK, :lanes] = now[0].astype(jnp.bfloat16)
                rhs[at : at + BLOCK, lanes:] = (-now[1]).astype(jnp.bfloat16)
                now = cmul(now, step_v)
        total_r = jnp.zeros((BLOCK, lanes), jnp.float32)
        total_i = jnp.zeros((BLOCK, lanes), jnp.float32)
        for a in range(down):
            for b in range(across):
                for part in range(2):
                    cs[a, part * side : (part + 1) * side, b * ALIGNED : b * ALIGNED + side] = c_ref[
                        a * across + b, j, part
                    ]
            res = jnp.dot(cs[a], rhs[...], preferred_element_type=jnp.float32)
            k = (lines + (first_row + a * stride)).astype(jnp.float32)
            now = cis(turns(k, wu))
            for h in range(side // BLOCK):
                top = res[h * BLOCK : (h + 1) * BLOCK]
                low = res[side + h * BLOCK : side + (h + 1) * BLOCK]
                inner_r = top[:, :lanes] - low[:, lanes:]
                inner_i = top[:, lanes:] + low[:, :lanes]
                total_r = total_r + (now[0] * inner_r + now[1] * inner_i)
                total_i = total_i + (now[0] * inner_i - now[1] * inner_r)
                now = cmul(now, step_u)
        put(
            j,
            jnp.sum(total_r, axis=0, keepdims=True) * (1.0 / SUBGRID),
            jnp.sum(total_i, axis=0, keepdims=True) * (1.0 / SUBGRID),
        )


def model_kernel(per_group, c_ref, uv_ref, out_ref, cs, rhs):
    facet_here = lax.axis_index("facet")

    def put(j, real, imaginary):
        out_ref[j, 0:1, :] = real
        out_ref[j, 1:2, :] = imaginary

    partial_models(
        facet_here,
        per_group,
        c_ref,
        lambda j: uv_ref[j, 0:1, :],
        lambda j: uv_ref[j, 1:2, :],
        put,
        cs,
        rhs,
    )


def grid_kernel(per_group, side, gain, off_ref, all_ref, out_ref, acc, left, right):
    columns, depth, lanes = all_ref.shape
    members = depth // 4
    rows = out_ref.shape[2]
    stride = (SUBGRID - side) // (FACET_SIDE - 1)
    span = right.shape[0]
    facet_here = lax.axis_index("facet")
    first_line = lax.axis_index("sub") * rows
    facet_rows = -(-per_group // 8) * 8
    corner_r, corner_c = corner(row_iota(facet_rows, lanes) + facet_here * per_group, stride)
    lines8 = row_iota(8, lanes)
    lines = row_iota(BLOCK, lanes)
    acc[...] = jnp.zeros_like(acc)

    def wide(x, n):
        return tuple(jnp.broadcast_to(t, (n, lanes)) for t in x)

    def line(x, at):
        return tuple(t[at : at + 1] for t in x)

    def join(x, step):
        y = cmul(x, step)
        return tuple(jnp.concatenate([p, q], axis=0) for p, q in zip(x, y))

    @pl.loop(0, columns * members)
    def _(s):
        column = lax.div(s, members)
        j = lax.rem(s, members)
        off_r = off_ref[column, j, 0]
        off_c = off_ref[column, j, 1]
        start = lax.rem(first_line - off_r + WIN, WIN)
        start = jnp.where(start > WIN - rows, start - WIN, start)
        tile = lax.div(off_c, BLOCK) * BLOCK
        shift = off_c - tile

        @pl.when(start < side)
        def _():
            wu = all_ref[column, pl.ds(j, 1), :] * (1.0 / SUBGRID)
            wv = all_ref[column, pl.ds(members + j, 1), :] * (1.0 / SUBGRID)
            rr = all_ref[column, pl.ds(2 * members + j, 1), :] * gain
            ri = all_ref[column, pl.ds(3 * members + j, 1), :] * gain
            lead = cis(
                turns((corner_r + start).astype(jnp.float32), wu)
                + turns((corner_c - shift).astype(jnp.float32), wv)
            )
            lead = cmul(lead, (rr, ri))
            jumps_u = cis(turns(((lines8 + 1) * 8).astype(jnp.float32), wu))
            jumps_v = cis(turns(((lines8 + 1) * 8).astype(jnp.float32), wv))
            base_u = cis(turns(lines8.astype(jnp.float32), wu))
            base_v = cis(turns(lines8.astype(jnp.float32), wv))

            now = join(base_v, wide(line(jumps_v, 0), 8))
            step = wide(line(jumps_v, 1), BLOCK)
            for h in range(span // BLOCK):
                cell = lines + (h * BLOCK - shift)
                live = (cell >= 0) & (cell < side)
                at = h * BLOCK
                right[at : at + BLOCK, :lanes] = jnp.where(live, now[0], 0.0).astype(jnp.bfloat16)
                right[at : at + BLOCK, lanes:] = jnp.where(live, now[1], 0.0).astype(jnp.bfloat16)
                now = cmul(now, step)

            tall = min(rows, BLOCK)
            now = base_u if tall == 8 else join(base_u, wide(line(jumps_u, 0), 8))
            step = wide(line(jumps_u, 0 if tall == 8 else 1), tall)
            ladder = row_iota(tall, lanes)
            for h in range(rows // tall):
                cell = ladder + (h * tall + start)
                live = (cell >= 0) & (cell < side)
                masked = tuple(jnp.where(live, t, 0.0) for t in now)
                for f in range(per_group):
                    value = cmul(masked, wide(line(lead, f), tall))
                    at = 2 * f * rows + h * tall
                    real = value[0].astype(jnp.bfloat16)
                    left[at : at + tall, :lanes] = real
                    left[at + rows : at + rows + tall, lanes:] = real
                    left[at + rows : at + rows + tall, :lanes] = value[1].astype(jnp.bfloat16)
                    left[at : at + tall, lanes:] = (-value[1]).astype(jnp.bfloat16)
                now = cmul(now, step)

            where = pl.ds(pl.multiple_of(tile, BLOCK), span)
            acc[where, :] += lax.dot_general(
                right[...],
                left[...],
                (((1,), (1,)), ((), ())),
                preferred_element_type=jnp.float32,
            )

    spill = acc.shape[0] - WIN
    acc[:spill, :] += acc[WIN:, :]
    folded = acc[:WIN, :].T
    for f in range(per_group):
        for part in range(2):
            at = (2 * f + part) * rows
            out_ref[f, part] = folded[at : at + rows]


def model_call(contributions, uv):
    per_group, members, _, side, _ = contributions.shape
    lanes = uv.shape[-1]
    across = min(per_group, FACET_SIDE)
    return pl.pallas_call(
        functools.partial(model_kernel, per_group),
        out_shape=jax.ShapeDtypeStruct((members, 2, lanes), jnp.float32),
        in_specs=[pl.BlockSpec(memory_space=pltpu.VMEM)] * 2,
        out_specs=pl.BlockSpec(memory_space=pltpu.VMEM),
        scratch_shapes=[
            pltpu.VMEM((per_group // across, 2 * side, across * ALIGNED), jnp.bfloat16),
            pltpu.VMEM((across * ALIGNED, 2 * lanes), jnp.bfloat16),
        ],
    )(contributions, uv)


def grid_call(offsets, gathered, per_group, side, rows, gain):
    lanes = gathered.shape[-1]
    span = side + BLOCK
    width = 2 * per_group * rows
    return pl.pallas_call(
        functools.partial(grid_kernel, per_group, side, gain),
        out_shape=jax.ShapeDtypeStruct((per_group, 2, rows, WIN), jnp.float32),
        in_specs=[
            pl.BlockSpec(memory_space=pltpu.SMEM),
            pl.BlockSpec(memory_space=pltpu.VMEM),
        ],
        out_specs=pl.BlockSpec(memory_space=pltpu.VMEM),
        scratch_shapes=[
            pltpu.VMEM((WIN + side, width), jnp.float32),
            pltpu.VMEM((width, 2 * lanes), jnp.bfloat16),
            pltpu.VMEM((span, 2 * lanes), jnp.bfloat16),
        ],
    )(offsets, gathered)


def body(contributions, slot_subgrid, vis_count, vis_uv, vis_obs, vis_weight, subgrid_offset):
    columns = lax.axis_size("sub")
    per_group, _, members, _, side, _ = contributions.shape
    lanes = vis_weight.shape[-1]
    slots = vis_weight.shape[2]
    packed = jnp.concatenate(
        [
            vis_uv[0, 0],
            vis_obs[0, 0],
            vis_weight[0, 0][:, None],
            jnp.broadcast_to(vis_count[0, 0].astype(jnp.float32)[:, None, None], (slots, 1, lanes)),
        ],
        axis=1,
    )
    packed = lax.all_gather(packed, "facet", axis=0, tiled=True)
    table = slot_subgrid[0].reshape(-1)
    picked = jnp.stack(
        [
            jnp.sum(jnp.where((table == j)[:, None, None], packed, 0.0), axis=0)
            for j in range(members)
        ]
    )
    part = model_call(contributions[:, 0], picked[:, :2])
    model = lax.psum(part, "facet")
    live = jnp.arange(lanes, dtype=jnp.float32)[None, None, :] < picked[:, 5:6]
    resid = jnp.where(live, picked[:, 4:5] * (picked[:, 2:4] - model), 0.0)
    resid = resid.astype(jnp.bfloat16).astype(jnp.float32)
    mine = jnp.concatenate([picked[:, 0], picked[:, 1], resid[:, 0], resid[:, 1]], axis=0)
    gathered = lax.all_gather(mine, "sub", axis=0)
    offsets = lax.all_gather(subgrid_offset[0], "sub", axis=0)
    gain = WIN / (side * math.sqrt(members * columns)) / math.sqrt(lanes)
    return grid_call(offsets, gathered, per_group, side, WIN // columns, gain)


def solution(mesh):
    placed = (
        P("facet", "sub", None, None, None, None),
        P("sub", None, None),
        P("facet", "sub", None),
        P("facet", "sub", None, None, None),
        P("facet", "sub", None, None, None),
        P("facet", "sub", None, None),
        P("sub", None, None),
    )
    return jax.shard_map(
        body, mesh=mesh, in_specs=placed, out_specs=P("facet", None, "sub", None), check_vma=False
    )
```

```python
import functools
import math

import jax
import jax.numpy as jnp
from jax import lax
from jax.experimental import pallas as pl
from jax.experimental.pallas import tpu as pltpu
from jax.sharding import PartitionSpec as P

SUBGRID = 512
FACET_SIDE = 4
WIN = 512
BLOCK = 16
ALIGNED = 256
MESH = pl.DeviceIdType.MESH


def cis(turn):
    turn = turn - jnp.floor(turn + 0.5)
    x = turn * math.pi
    q = x * x
    s = -1.0 / math.factorial(11)
    for order in (9, 7, 5, 3, 1):
        sign = 1.0 if order % 4 == 1 else -1.0
        s = s * q + sign / math.factorial(order)
    s = s * x
    c = 1.0 / math.factorial(12)
    for order in (10, 8, 6, 4, 2, 0):
        sign = 1.0 if order % 4 == 0 else -1.0
        c = c * q + sign / math.factorial(order)
    return 1.0 - 2.0 * s * s, 2.0 * s * c


def turns(k, w):
    high = jnp.floor(w * 4096.0) * (1.0 / 4096.0)
    low = w - high
    p = k * high
    return (p - jnp.floor(p + 0.5)) + k * low


def cmul(a, b):
    return a[0] * b[0] - a[1] * b[1], a[0] * b[1] + a[1] * b[0]


def row_iota(rows, lanes):
    return lax.broadcasted_iota(jnp.int32, (rows, lanes), 0)


def corner(index, stride):
    return lax.div(index, FACET_SIDE) * stride, lax.rem(index, FACET_SIDE) * stride


def partial_models(facet_here, per_group, first, number, c_ref, u_of, v_of, put, cs, rhs):
    side = c_ref.shape[-1]
    stride = (SUBGRID - side) // (FACET_SIDE - 1)
    across = min(per_group, FACET_SIDE)
    down = per_group // across
    lanes = rhs.shape[1] // 2
    first_row, first_col = corner(facet_here * per_group, stride)
    lines = row_iota(BLOCK, lanes)

    @pl.loop(first, first + number)
    def _(j):
        wu = u_of(j) * (1.0 / SUBGRID)
        wv = v_of(j) * (1.0 / SUBGRID)
        step_v = tuple(jnp.broadcast_to(t, (BLOCK, lanes)) for t in cis(turns(float(BLOCK), wv)))
        step_u = tuple(jnp.broadcast_to(t, (BLOCK, lanes)) for t in cis(turns(float(BLOCK), wu)))
        for b in range(across):
            k = (lines + (first_col + b * stride)).astype(jnp.float32)
            now = cis(turns(k, wv))
            for h in range(side // BLOCK):
                at = b * ALIGNED + h * BLOCK
                rhs[at : at + BLOCK, :lanes] = now[0].astype(jnp.bfloat16)
                rhs[at : at + BLOCK, lanes:] = (-now[1]).astype(jnp.bfloat16)
                now = cmul(now, step_v)
        total_r = jnp.zeros((BLOCK, lanes), jnp.float32)
        total_i = jnp.zeros((BLOCK, lanes), jnp.float32)
        for a in range(down):
            for b in range(across):
                for part in range(2):
                    cs[a, part * side : (part + 1) * side, b * ALIGNED : b * ALIGNED + side] = c_ref[
                        a * across + b, j, part
                    ]
            res = jnp.dot(cs[a], rhs[...], preferred_element_type=jnp.float32)
            k = (lines + (first_row + a * stride)).astype(jnp.float32)
            now = cis(turns(k, wu))
            for h in range(side // BLOCK):
                top = res[h * BLOCK : (h + 1) * BLOCK]
                low = res[side + h * BLOCK : side + (h + 1) * BLOCK]
                inner_r = top[:, :lanes] - low[:, lanes:]
                inner_i = top[:, lanes:] + low[:, :lanes]
                total_r = total_r + (now[0] * inner_r + now[1] * inner_i)
                total_i = total_i + (now[0] * inner_i - now[1] * inner_r)
                now = cmul(now, step_u)
        put(
            j,
            jnp.sum(total_r, axis=0, keepdims=True) * (1.0 / SUBGRID),
            jnp.sum(total_i, axis=0, keepdims=True) * (1.0 / SUBGRID),
        )


def exchange_kernel(
    groups,
    columns,
    per_group,
    table_ref,
    count_ref,
    off_ref,
    c_hbm,
    uv_ref,
    obs_ref,
    weight_ref,
    all_ref,
    where_ref,
    c_ref,
    cs,
    rhs,
    uv_all,
    ow_all,
    ow_mine,
    uv_mine,
    uv_cols,
    part_mine,
    part_all,
    resid_mine,
    resid_cols,
    c_sem,
    uv_send,
    uv_recv,
    ow_send,
    ow_recv,
    cols_send,
    cols_recv,
    part_send,
    part_recv,
    resid_send,
    resid_recv,
):
    members = c_ref.shape[1]
    slots = uv_ref.shape[2]
    lanes = uv_ref.shape[-1]
    halves = part_send.shape[0]
    each = members // halves
    group = lax.axis_index("facet")
    column = lax.axis_index("sub")
    loads = [
        pltpu.make_async_copy(c_hbm.at[:, 0, j], c_ref.at[:, j], c_sem.at[j]) for j in range(members)
    ]
    for load in loads:
        load.start()

    barrier = pltpu.get_barrier_semaphore()

    def peer_group(p):
        return lax.rem(group + p, groups)

    def peer_column(p):
        return lax.rem(column + p, columns)

    @pl.loop(1, groups)
    def _(p):
        pl.semaphore_signal(barrier, inc=1, device_id={"facet": peer_group(p)}, device_id_type=MESH)

    @pl.loop(1, columns)
    def _(p):
        pl.semaphore_signal(barrier, inc=1, device_id={"sub": peer_column(p)}, device_id_type=MESH)

    lane = lax.broadcasted_iota(jnp.int32, (1, lanes), 1)
    for k in range(slots):
        ow_mine[k, 0:2, :] = obs_ref[0, 0, k]
        live = jnp.where(lane < count_ref[0, 0, k], 1.0, 0.0)
        ow_mine[k, 2:3, :] = weight_ref[0, 0, k : k + 1, :] * live
    uv_all[group] = uv_ref[0, 0]
    ow_all[group] = ow_mine[...]
    cs[...] = jnp.zeros_like(cs)
    rhs[...] = jnp.zeros_like(rhs)
    pl.semaphore_wait(barrier, groups - 1 + columns - 1)

    def to_group(src, dst, send, recv, p):
        return pltpu.make_async_remote_copy(
            src_ref=src,
            dst_ref=dst,
            send_sem=send.at[p],
            recv_sem=recv.at[p],
            device_id={"facet": peer_group(p)},
            device_id_type=MESH,
        )

    def to_column(src, dst, send, recv, p):
        return pltpu.make_async_remote_copy(
            src_ref=src,
            dst_ref=dst,
            send_sem=send.at[p],
            recv_sem=recv.at[p],
            device_id={"sub": peer_column(p)},
            device_id_type=MESH,
        )

    def each_group(make, act):
        @pl.loop(1, groups)
        def _(p):
            act(make(p))

    def each_column(make, act):
        @pl.loop(1, columns)
        def _(p):
            act(make(p))

    def uv_copy(p):
        return to_group(uv_ref.at[0, 0], uv_all.at[group], uv_send, uv_recv, p)

    def ow_copy(p):
        return to_group(ow_mine, ow_all.at[group], ow_send, ow_recv, p)

    def cols_copy(p):
        return to_column(uv_mine, uv_cols.at[column], cols_send, cols_recv, p)

    def part_copy(h):
        return lambda p: to_group(
            part_mine.at[h], part_all.at[h, group], part_send.at[h], part_recv.at[h], p
        )

    def resid_copy(h):
        return lambda p: to_column(
            resid_mine.at[h], resid_cols.at[column, h], resid_send.at[h], resid_recv.at[h], p
        )

    def start(copy):
        copy.start()

    def wait(copy):
        copy.wait()

    each_group(uv_copy, start)
    each_group(ow_copy, start)
    each_group(uv_copy, wait)

    def holds(g, k, j):
        return jnp.where(table_ref[0, g, k] == j, 1.0, 0.0)

    @pl.loop(0, members)
    def _(j):
        picked = jnp.zeros((2, lanes), jnp.float32)
        for g in range(groups):
            for k in range(slots):
                picked = picked + uv_all[g, k] * holds(g, k, j)
        uv_mine[j, 0:2, :] = picked
        uv_mine[j, 2:3, :] = jnp.where(
            lane == 0, off_ref[0, j, 0], jnp.where(lane == 1, off_ref[0, j, 1], 0)
        ).astype(jnp.float32)

    uv_cols[column] = uv_mine[...]
    each_column(cols_copy, start)
    for load in loads:
        load.wait()

    for h in range(halves):

        def put(j, real, imaginary):
            part_mine[h, j - h * each, 0:1, :] = real
            part_mine[h, j - h * each, 1:2, :] = imaginary

        partial_models(
            group,
            per_group,
            h * each,
            each,
            c_ref,
            lambda j: uv_mine[j, 0:1, :],
            lambda j: uv_mine[j, 1:2, :],
            put,
            cs,
            rhs,
        )
        part_all[h, group] = part_mine[h]
        each_group(part_copy(h), start)

    each_group(ow_copy, wait)
    for h in range(halves):
        each_group(part_copy(h), wait)

        @pl.loop(0, each)
        def _(i):
            picked = jnp.zeros((3, lanes), jnp.float32)
            model = jnp.zeros((2, lanes), jnp.float32)
            for g in range(groups):
                model = model + part_all[h, g, i]
                for k in range(slots):
                    picked = picked + ow_all[g, k] * holds(g, k, h * each + i)
            resid = picked[2:3] * (picked[0:2] - model)
            resid_mine[h, i] = resid.astype(jnp.bfloat16)

        resid_cols[column, h] = resid_mine[h]
        each_column(resid_copy(h), start)

    each_column(cols_copy, wait)

    @pl.loop(0, columns)
    def _(c):
        for j in range(members):
            all_ref[c, j : j + 1, :] = uv_cols[c, j, 0:1, :]
            all_ref[c, members + j : members + j + 1, :] = uv_cols[c, j, 1:2, :]
            where_ref[c, j : j + 1, :] = uv_cols[c, j, 2:3, :128].astype(jnp.int32)

    for h in range(halves):
        each_column(resid_copy(h), wait)

    @pl.loop(0, columns)
    def _(c):
        for j in range(members):
            resid = resid_cols[c, j // each, j % each].astype(jnp.float32)
            all_ref[c, 2 * members + j : 2 * members + j + 1, :] = resid[0:1]
            all_ref[c, 3 * members + j : 3 * members + j + 1, :] = resid[1:2]


def grid_kernel(per_group, side, gain, off_ref, all_ref, out_ref, acc, left, right):
    columns, depth, lanes = all_ref.shape
    members = depth // 4
    rows = out_ref.shape[2]
    stride = (SUBGRID - side) // (FACET_SIDE - 1)
    span = right.shape[0]
    facet_here = lax.axis_index("facet")
    first_line = lax.axis_index("sub") * rows
    facet_rows = -(-per_group // 8) * 8
    corner_r, corner_c = corner(row_iota(facet_rows, lanes) + facet_here * per_group, stride)
    lines8 = row_iota(8, lanes)
    lines = row_iota(BLOCK, lanes)
    acc[...] = jnp.zeros_like(acc)

    def wide(x, n):
        return tuple(jnp.broadcast_to(t, (n, lanes)) for t in x)

    def line(x, at):
        return tuple(t[at : at + 1] for t in x)

    def join(x, step):
        y = cmul(x, step)
        return tuple(jnp.concatenate([p, q], axis=0) for p, q in zip(x, y))

    @pl.loop(0, columns * members)
    def _(s):
        column = lax.div(s, members)
        j = lax.rem(s, members)
        off_r = off_ref[column, j, 0]
        off_c = off_ref[column, j, 1]
        start = lax.rem(first_line - off_r + WIN, WIN)
        start = jnp.where(start > WIN - rows, start - WIN, start)
        tile = lax.div(off_c, BLOCK) * BLOCK
        shift = off_c - tile

        @pl.when(start < side)
        def _():
            wu = all_ref[column, pl.ds(j, 1), :] * (1.0 / SUBGRID)
            wv = all_ref[column, pl.ds(members + j, 1), :] * (1.0 / SUBGRID)
            rr = all_ref[column, pl.ds(2 * members + j, 1), :] * gain
            ri = all_ref[column, pl.ds(3 * members + j, 1), :] * gain
            lead = cis(
                turns((corner_r + start).astype(jnp.float32), wu)
                + turns((corner_c - shift).astype(jnp.float32), wv)
            )
            lead = cmul(lead, (rr, ri))
            jumps_u = cis(turns(((lines8 + 1) * 8).astype(jnp.float32), wu))
            jumps_v = cis(turns(((lines8 + 1) * 8).astype(jnp.float32), wv))
            base_u = cis(turns(lines8.astype(jnp.float32), wu))
            base_v = cis(turns(lines8.astype(jnp.float32), wv))

            now = join(base_v, wide(line(jumps_v, 0), 8))
            step = wide(line(jumps_v, 1), BLOCK)
            for h in range(span // BLOCK):
                cell = lines + (h * BLOCK - shift)
                live = (cell >= 0) & (cell < side)
                at = h * BLOCK
                right[at : at + BLOCK, :lanes] = jnp.where(live, now[0], 0.0).astype(jnp.bfloat16)
                right[at : at + BLOCK, lanes:] = jnp.where(live, now[1], 0.0).astype(jnp.bfloat16)
                now = cmul(now, step)

            tall = min(rows, BLOCK)
            now = base_u if tall == 8 else join(base_u, wide(line(jumps_u, 0), 8))
            step = wide(line(jumps_u, 0 if tall == 8 else 1), tall)
            ladder = row_iota(tall, lanes)
            for h in range(rows // tall):
                cell = ladder + (h * tall + start)
                live = (cell >= 0) & (cell < side)
                masked = tuple(jnp.where(live, t, 0.0) for t in now)
                for f in range(per_group):
                    value = cmul(masked, wide(line(lead, f), tall))
                    at = 2 * f * rows + h * tall
                    real = value[0].astype(jnp.bfloat16)
                    left[at : at + tall, :lanes] = real
                    left[at + rows : at + rows + tall, lanes:] = real
                    left[at + rows : at + rows + tall, :lanes] = value[1].astype(jnp.bfloat16)
                    left[at : at + tall, lanes:] = (-value[1]).astype(jnp.bfloat16)
                now = cmul(now, step)

            where = pl.ds(pl.multiple_of(tile, BLOCK), span)
            acc[where, :] += lax.dot_general(
                right[...],
                left[...],
                (((1,), (1,)), ((), ())),
                preferred_element_type=jnp.float32,
            )

    spill = acc.shape[0] - WIN
    acc[:spill, :] += acc[WIN:, :]
    folded = acc[:WIN, :].T
    for f in range(per_group):
        for part in range(2):
            at = (2 * f + part) * rows
            out_ref[f, part] = folded[at : at + rows]


def exchange_call(groups, columns, slot_subgrid, vis_count, offset, contributions, uv, obs, weight):
    per_group, _, members, _, side, _ = contributions.shape
    slots, lanes = weight.shape[2:]
    across = min(per_group, FACET_SIDE)
    halves = 2 if members % 2 == 0 else 1
    each = members // halves
    smem = pl.BlockSpec(memory_space=pltpu.SMEM)
    vmem = pl.BlockSpec(memory_space=pltpu.VMEM)
    dma = pltpu.SemaphoreType.DMA
    f32, bf16 = jnp.float32, jnp.bfloat16
    return pl.pallas_call(
        functools.partial(exchange_kernel, groups, columns, per_group),
        out_shape=(
            jax.ShapeDtypeStruct((columns, 4 * members, lanes), f32),
            jax.ShapeDtypeStruct((columns, members, 128), jnp.int32),
        ),
        in_specs=[smem, smem, smem, pl.BlockSpec(memory_space=pl.ANY), vmem, vmem, vmem],
        out_specs=(vmem, vmem),
        scratch_shapes=[
            pltpu.VMEM((per_group, members, 2, side, side), bf16),
            pltpu.VMEM((per_group // across, 2 * side, across * ALIGNED), bf16),
            pltpu.VMEM((across * ALIGNED, 2 * lanes), bf16),
            pltpu.VMEM((groups, slots, 2, lanes), f32),
            pltpu.VMEM((groups, slots, 3, lanes), f32),
            pltpu.VMEM((slots, 3, lanes), f32),
            pltpu.VMEM((members, 3, lanes), f32),
            pltpu.VMEM((columns, members, 3, lanes), f32),
            pltpu.VMEM((halves, each, 2, lanes), f32),
            pltpu.VMEM((halves, groups, each, 2, lanes), f32),
            pltpu.VMEM((halves, each, 2, lanes), bf16),
            pltpu.VMEM((columns, halves, each, 2, lanes), bf16),
            dma((members,)),
            dma((groups,)),
            dma((groups,)),
            dma((groups,)),
            dma((groups,)),
            dma((columns,)),
            dma((columns,)),
            dma((halves, groups)),
            dma((halves, groups)),
            dma((halves, columns)),
            dma((halves, columns)),
        ],
        compiler_params=pltpu.CompilerParams(collective_id=0, has_side_effects=True),
    )(slot_subgrid, vis_count, offset, contributions, uv, obs, weight)


def grid_call(offsets, gathered, per_group, side, rows, gain):
    lanes = gathered.shape[-1]
    span = side + BLOCK
    width = 2 * per_group * rows
    return pl.pallas_call(
        functools.partial(grid_kernel, per_group, side, gain),
        out_shape=jax.ShapeDtypeStruct((per_group, 2, rows, WIN), jnp.float32),
        in_specs=[
            pl.BlockSpec(memory_space=pltpu.SMEM),
            pl.BlockSpec(memory_space=pltpu.VMEM),
        ],
        out_specs=pl.BlockSpec(memory_space=pltpu.VMEM),
        scratch_shapes=[
            pltpu.VMEM((WIN + side, width), jnp.float32),
            pltpu.VMEM((width, 2 * lanes), jnp.bfloat16),
            pltpu.VMEM((span, 2 * lanes), jnp.bfloat16),
        ],
    )(offsets, gathered)


def body(contributions, slot_subgrid, vis_count, vis_uv, vis_obs, vis_weight, subgrid_offset):
    groups = lax.axis_size("facet")
    columns = lax.axis_size("sub")
    per_group, _, members, _, side, _ = contributions.shape
    lanes = vis_weight.shape[-1]
    gathered, offsets = exchange_call(
        groups,
        columns,
        slot_subgrid,
        vis_count,
        subgrid_offset,
        contributions,
        vis_uv,
        vis_obs,
        vis_weight,
    )
    gain = WIN / (side * math.sqrt(members * columns)) / math.sqrt(lanes)
    return grid_call(offsets, gathered, per_group, side, WIN // columns, gain)


def solution(mesh):
    placed = (
        P("facet", "sub", None, None, None, None),
        P("sub", None, None),
        P("facet", "sub", None),
        P("facet", "sub", None, None, None),
        P("facet", "sub", None, None, None),
        P("facet", "sub", None, None),
        P("sub", None, None),
    )
    return jax.shard_map(
        body, mesh=mesh, in_specs=placed, out_specs=P("facet", None, "sub", None), check_vma=False
    )
```

```python
import functools
import math

import jax
import jax.numpy as jnp
from jax import lax
from jax.experimental import pallas as pl
from jax.experimental.pallas import tpu as pltpu
from jax.sharding import PartitionSpec as P

SUBGRID = 512
FACET_SIDE = 4
WIN = 512
BLOCK = 16
MESH = pl.DeviceIdType.MESH


def cis(turn):
    turn = turn - jnp.floor(turn + 0.5)
    x = turn * math.pi
    q = x * x
    s = -1.0 / math.factorial(11)
    for order in (9, 7, 5, 3, 1):
        sign = 1.0 if order % 4 == 1 else -1.0
        s = s * q + sign / math.factorial(order)
    s = s * x
    c = 1.0 / math.factorial(12)
    for order in (10, 8, 6, 4, 2, 0):
        sign = 1.0 if order % 4 == 0 else -1.0
        c = c * q + sign / math.factorial(order)
    return 1.0 - 2.0 * s * s, 2.0 * s * c


def turns(k, w):
    high = jnp.floor(w * 4096.0) * (1.0 / 4096.0)
    low = w - high
    p = k * high
    return (p - jnp.floor(p + 0.5)) + k * low


def cmul(a, b):
    return a[0] * b[0] - a[1] * b[1], a[0] * b[1] + a[1] * b[0]


def row_iota(rows, lanes):
    return lax.broadcasted_iota(jnp.int32, (rows, lanes), 0)


def corner(index, stride):
    return lax.div(index, FACET_SIDE) * stride, lax.rem(index, FACET_SIDE) * stride


def blocks_in(c_ref, cs, j):
    per_group, _, _, side, _ = c_ref.shape
    across = min(per_group, FACET_SIDE)
    for a in range(per_group // across):
        for part in range(2):
            strip = jnp.concatenate([c_ref[a * across + b, j, part] for b in range(across)], axis=1)
            cs[j, a, part * side : (part + 1) * side, :] = strip


def column_tables(first_col, stride, side, v, rhs):
    lanes = rhs.shape[1] // 2
    lines = row_iota(BLOCK, lanes)
    wv = v * (1.0 / SUBGRID)
    step = tuple(jnp.broadcast_to(t, (BLOCK, lanes)) for t in cis(turns(float(BLOCK), wv)))
    for b in range(rhs.shape[0] // side):
        k = (lines + (first_col + b * stride)).astype(jnp.float32)
        now = cis(turns(k, wv))
        for h in range(side // BLOCK):
            at = b * side + h * BLOCK
            rhs[at : at + BLOCK, :lanes] = now[0].astype(jnp.bfloat16)
            rhs[at : at + BLOCK, lanes:] = (-now[1]).astype(jnp.bfloat16)
            now = cmul(now, step)


def partial_model(first_row, stride, side, u, images, rhs):
    lanes = rhs.shape[1] // 2
    lines = row_iota(BLOCK, lanes)
    wu = u * (1.0 / SUBGRID)
    step = tuple(jnp.broadcast_to(t, (BLOCK, lanes)) for t in cis(turns(float(BLOCK), wu)))
    total_r = jnp.zeros((BLOCK, lanes), jnp.float32)
    total_i = jnp.zeros((BLOCK, lanes), jnp.float32)
    for a in range(images.shape[0]):
        res = jnp.dot(images[a], rhs[...], preferred_element_type=jnp.float32)
        k = (lines + (first_row + a * stride)).astype(jnp.float32)
        now = cis(turns(k, wu))
        for h in range(side // BLOCK):
            top = res[h * BLOCK : (h + 1) * BLOCK]
            low = res[side + h * BLOCK : side + (h + 1) * BLOCK]
            inner_r = top[:, :lanes] - low[:, lanes:]
            inner_i = top[:, lanes:] + low[:, :lanes]
            total_r = total_r + (now[0] * inner_r + now[1] * inner_i)
            total_i = total_i + (now[0] * inner_i - now[1] * inner_r)
            now = cmul(now, step)
    return (
        jnp.sum(total_r, axis=0, keepdims=True) * (1.0 / SUBGRID),
        jnp.sum(total_i, axis=0, keepdims=True) * (1.0 / SUBGRID),
    )


def exchange_kernel(
    groups,
    columns,
    per_group,
    table_ref,
    count_ref,
    off_ref,
    c_hbm,
    uv_ref,
    obs_ref,
    weight_ref,
    all_ref,
    where_ref,
    c_ref,
    cs,
    rhs,
    uv_all,
    ow_all,
    ow_mine,
    uv_mine,
    uv_cols,
    part_mine,
    part_all,
    resid_mine,
    resid_cols,
    c_sem,
    uv_send,
    uv_recv,
    ow_send,
    ow_recv,
    cols_send,
    cols_recv,
    part_send,
    part_recv,
    resid_send,
    resid_recv,
):
    members = c_ref.shape[1]
    slots = uv_ref.shape[2]
    lanes = uv_ref.shape[-1]
    halves = part_send.shape[0]
    each = members // halves
    group = lax.axis_index("facet")
    column = lax.axis_index("sub")
    loads = [
        pltpu.make_async_copy(c_hbm.at[:, 0, j], c_ref.at[:, j], c_sem.at[j]) for j in range(members)
    ]
    for load in loads:
        load.start()

    barrier = pltpu.get_barrier_semaphore()

    def peer_group(p):
        return lax.rem(group + p, groups)

    def peer_column(p):
        return lax.rem(column + p, columns)

    @pl.loop(1, groups)
    def _(p):
        pl.semaphore_signal(barrier, inc=1, device_id={"facet": peer_group(p)}, device_id_type=MESH)

    @pl.loop(1, columns)
    def _(p):
        pl.semaphore_signal(barrier, inc=1, device_id={"sub": peer_column(p)}, device_id_type=MESH)

    lane = lax.broadcasted_iota(jnp.int32, (1, lanes), 1)
    for k in range(slots):
        ow_mine[k, 0:2, :] = obs_ref[0, 0, k]
        live = jnp.where(lane < count_ref[0, 0, k], 1.0, 0.0)
        ow_mine[k, 2:3, :] = weight_ref[0, 0, k : k + 1, :] * live
    uv_all[group] = uv_ref[0, 0]
    ow_all[group] = ow_mine[...]
    pl.semaphore_wait(barrier, groups - 1 + columns - 1)

    def to_group(src, dst, send, recv, p):
        return pltpu.make_async_remote_copy(
            src_ref=src,
            dst_ref=dst,
            send_sem=send.at[p],
            recv_sem=recv.at[p],
            device_id={"facet": peer_group(p)},
            device_id_type=MESH,
        )

    def to_column(src, dst, send, recv, p):
        return pltpu.make_async_remote_copy(
            src_ref=src,
            dst_ref=dst,
            send_sem=send.at[p],
            recv_sem=recv.at[p],
            device_id={"sub": peer_column(p)},
            device_id_type=MESH,
        )

    def each_group(make, act):
        @pl.loop(1, groups)
        def _(p):
            act(make(p))

    def each_column(make, act):
        @pl.loop(1, columns)
        def _(p):
            act(make(p))

    def uv_copy(p):
        return to_group(uv_ref.at[0, 0], uv_all.at[group], uv_send, uv_recv, p)

    def ow_copy(p):
        return to_group(ow_mine, ow_all.at[group], ow_send, ow_recv, p)

    def cols_copy(p):
        return to_column(uv_mine, uv_cols.at[column], cols_send, cols_recv, p)

    def part_copy(h):
        return lambda p: to_group(
            part_mine.at[h], part_all.at[h, group], part_send.at[h], part_recv.at[h], p
        )

    def resid_copy(h):
        return lambda p: to_column(
            resid_mine.at[h], resid_cols.at[column, h], resid_send.at[h], resid_recv.at[h], p
        )

    def start(copy):
        copy.start()

    def wait(copy):
        copy.wait()

    each_group(uv_copy, start)
    each_group(ow_copy, start)
    for load in loads:
        load.wait()

    @pl.loop(0, members)
    def _(j):
        blocks_in(c_ref, cs, j)

    each_group(uv_copy, wait)

    def holds(g, k, j):
        return jnp.where(table_ref[0, g, k] == j, 1.0, 0.0)

    @pl.loop(0, members)
    def _(j):
        picked = jnp.zeros((2, lanes), jnp.float32)
        for g in range(groups):
            for k in range(slots):
                picked = picked + uv_all[g, k] * holds(g, k, j)
        uv_mine[j, 0:2, :] = picked
        uv_mine[j, 2:3, :] = jnp.where(
            lane == 0, off_ref[0, j, 0], jnp.where(lane == 1, off_ref[0, j, 1], 0)
        ).astype(jnp.float32)

    uv_cols[column] = uv_mine[...]
    each_column(cols_copy, start)

    side = c_ref.shape[-1]
    stride = (SUBGRID - side) // (FACET_SIDE - 1)
    first_row, first_col = corner(group * per_group, stride)

    def tables(j, slot):
        column_tables(first_col, stride, side, uv_mine[j, 1:2, :], rhs[slot])

    def models(h, j, slot):
        real, imaginary = partial_model(
            first_row, stride, side, uv_mine[j, 0:1, :], cs.at[j], rhs[slot]
        )
        part_mine[h, j - h * each, 0:1, :] = real
        part_mine[h, j - h * each, 1:2, :] = imaginary

    if each == 1:
        tables(0, 0)
    for h in range(halves):
        if each == 1:
            if h + 1 < halves:
                tables(h + 1, (h + 1) % 2)
            models(h, h, h % 2)
        else:

            @pl.loop(h * each, (h + 1) * each)
            def _(j):
                tables(j, 0)
                models(h, j, 0)

        part_all[h, group] = part_mine[h]
        each_group(part_copy(h), start)

    each_group(ow_copy, wait)
    for h in range(halves):
        each_group(part_copy(h), wait)

        @pl.loop(0, each)
        def _(i):
            picked = jnp.zeros((3, lanes), jnp.float32)
            model = jnp.zeros((2, lanes), jnp.float32)
            for g in range(groups):
                model = model + part_all[h, g, i]
                for k in range(slots):
                    picked = picked + ow_all[g, k] * holds(g, k, h * each + i)
            resid = picked[2:3] * (picked[0:2] - model)
            resid_mine[h, i] = resid.astype(jnp.bfloat16)

        resid_cols[column, h] = resid_mine[h]
        each_column(resid_copy(h), start)

    each_column(cols_copy, wait)

    @pl.loop(0, columns)
    def _(c):
        for j in range(members):
            all_ref[c, j : j + 1, :] = uv_cols[c, j, 0:1, :]
            all_ref[c, members + j : members + j + 1, :] = uv_cols[c, j, 1:2, :]
            where_ref[c, j : j + 1, :] = uv_cols[c, j, 2:3, :128].astype(jnp.int32)

    for h in range(halves):
        each_column(resid_copy(h), wait)

    @pl.loop(0, columns)
    def _(c):
        for j in range(members):
            resid = resid_cols[c, j // each, j % each].astype(jnp.float32)
            all_ref[c, 2 * members + j : 2 * members + j + 1, :] = resid[0:1]
            all_ref[c, 3 * members + j : 3 * members + j + 1, :] = resid[1:2]


def grid_kernel(per_group, side, gain, off_ref, all_ref, out_ref, acc, lefts, rights, hits):
    columns, depth, lanes = all_ref.shape
    members = depth // 4
    rows = out_ref.shape[2]
    stride = (SUBGRID - side) // (FACET_SIDE - 1)
    span = rights[0].shape[0]
    facet_here = lax.axis_index("facet")
    first_line = lax.axis_index("sub") * rows
    facet_rows = -(-per_group // 8) * 8
    corner_r, corner_c = corner(row_iota(facet_rows, lanes) + facet_here * per_group, stride)
    lines8 = row_iota(8, lanes)
    lines = row_iota(BLOCK, lanes)
    acc[...] = jnp.zeros_like(acc)

    def wide(x, n):
        return tuple(jnp.broadcast_to(t, (n, lanes)) for t in x)

    def line(x, at):
        return tuple(t[at : at + 1] for t in x)

    def join(x, step):
        y = cmul(x, step)
        return tuple(jnp.concatenate([p, q], axis=0) for p, q in zip(x, y))

    def place(s):
        column = lax.div(s, members)
        j = lax.rem(s, members)
        start = lax.rem(first_line - off_ref[column, j, 0] + WIN, WIN)
        return column, j, jnp.where(start > WIN - rows, start - WIN, start)

    total = columns * members

    def scan(s, found):
        hits[found] = s
        return found + jnp.where(place(s)[2] < side, 1, 0)

    found = lax.fori_loop(0, total, scan, jnp.int32(0))

    def fill(index, left, right):
        s = jnp.where(index < found, hits[jnp.minimum(index, total - 1)], 0)
        scale = jnp.where(index < found, gain, 0.0)
        column, j, start = place(s)
        off_c = off_ref[column, j, 1]
        tile = lax.div(off_c, BLOCK) * BLOCK
        shift = off_c - tile
        wu = all_ref[column, pl.ds(j, 1), :] * (1.0 / SUBGRID)
        wv = all_ref[column, pl.ds(members + j, 1), :] * (1.0 / SUBGRID)
        rr = all_ref[column, pl.ds(2 * members + j, 1), :] * scale
        ri = all_ref[column, pl.ds(3 * members + j, 1), :] * scale
        lead = cis(
            turns((corner_r + start).astype(jnp.float32), wu)
            + turns((corner_c - shift).astype(jnp.float32), wv)
        )
        lead = cmul(lead, (rr, ri))
        jumps = cis(turns((lax.rem(lines8, 4) * 8).astype(jnp.float32), jnp.where(lines8 < 4, wu, wv)))
        base_u = cis(turns(lines8.astype(jnp.float32), wu))
        base_v = cis(turns(lines8.astype(jnp.float32), wv))

        now = join(base_v, wide(line(jumps, 5), 8))
        step = wide(line(jumps, 6), BLOCK)
        for h in range(span // BLOCK):
            shown = now
            if h == 0 or (h + 1) * BLOCK > side:
                cell = lines + (h * BLOCK - shift)
                live = (cell >= 0) & (cell < side)
                shown = tuple(jnp.where(live, t, 0.0) for t in now)
            at = h * BLOCK
            right[at : at + BLOCK, :lanes] = shown[0].astype(jnp.bfloat16)
            right[at : at + BLOCK, lanes:] = shown[1].astype(jnp.bfloat16)
            now = cmul(now, step)

        tall = min(rows, BLOCK)
        now = base_u if tall == 8 else join(base_u, wide(line(jumps, 1), 8))
        step = wide(line(jumps, 1 if tall == 8 else 2), tall)
        ladder = row_iota(tall, lanes)
        for h in range(rows // tall):
            cell = ladder + (h * tall + start)
            live = (cell >= 0) & (cell < side)
            masked = tuple(jnp.where(live, t, 0.0) for t in now)
            for f in range(per_group):
                value = cmul(masked, wide(line(lead, f), tall))
                at = 2 * f * rows + h * tall
                real = value[0].astype(jnp.bfloat16)
                left[at : at + tall, :lanes] = real
                left[at + rows : at + rows + tall, lanes:] = real
                left[at + rows : at + rows + tall, :lanes] = value[1].astype(jnp.bfloat16)
                left[at : at + tall, lanes:] = (-value[1]).astype(jnp.bfloat16)
            now = cmul(now, step)
        return tile

    def add(tile, left, right):
        where = pl.ds(pl.multiple_of(tile, BLOCK), span)
        acc[where, :] += lax.dot_general(
            right[...], left[...], (((1,), (1,)), ((), ())), preferred_element_type=jnp.float32
        )

    def pair(i, tile):
        later = fill(2 * i + 1, lefts[1], rights[1])
        add(tile, lefts[0], rights[0])
        tile = fill(2 * i + 2, lefts[0], rights[0])
        add(later, lefts[1], rights[1])
        return tile

    first = fill(0, lefts[0], rights[0])
    lax.fori_loop(0, lax.div(found + 1, 2), pair, first)

    spill = acc.shape[0] - WIN
    acc[:spill, :] += acc[WIN:, :]
    folded = acc[:WIN, :].T
    for f in range(per_group):
        for part in range(2):
            at = (2 * f + part) * rows
            out_ref[f, part] = folded[at : at + rows]


def exchange_call(groups, columns, slot_subgrid, vis_count, offset, contributions, uv, obs, weight):
    per_group, _, members, _, side, _ = contributions.shape
    slots, lanes = weight.shape[2:]
    across = min(per_group, FACET_SIDE)
    halves = 2 if members % 2 == 0 else 1
    each = members // halves
    smem = pl.BlockSpec(memory_space=pltpu.SMEM)
    vmem = pl.BlockSpec(memory_space=pltpu.VMEM)
    dma = pltpu.SemaphoreType.DMA
    f32, bf16 = jnp.float32, jnp.bfloat16
    return pl.pallas_call(
        functools.partial(exchange_kernel, groups, columns, per_group),
        out_shape=(
            jax.ShapeDtypeStruct((columns, 4 * members, lanes), f32),
            jax.ShapeDtypeStruct((columns, members, 128), jnp.int32),
        ),
        in_specs=[smem, smem, smem, pl.BlockSpec(memory_space=pl.ANY), vmem, vmem, vmem],
        out_specs=(vmem, vmem),
        scratch_shapes=[
            pltpu.VMEM((per_group, members, 2, side, side), bf16),
            pltpu.VMEM((members, per_group // across, 2 * side, across * side), bf16),
            [pltpu.VMEM((across * side, 2 * lanes), bf16)] * 2,
            pltpu.VMEM((groups, slots, 2, lanes), f32),
            pltpu.VMEM((groups, slots, 3, lanes), f32),
            pltpu.VMEM((slots, 3, lanes), f32),
            pltpu.VMEM((members, 3, lanes), f32),
            pltpu.VMEM((columns, members, 3, lanes), f32),
            pltpu.VMEM((halves, each, 2, lanes), f32),
            pltpu.VMEM((halves, groups, each, 2, lanes), f32),
            pltpu.VMEM((halves, each, 2, lanes), bf16),
            pltpu.VMEM((columns, halves, each, 2, lanes), bf16),
            dma((members,)),
            dma((groups,)),
            dma((groups,)),
            dma((groups,)),
            dma((groups,)),
            dma((columns,)),
            dma((columns,)),
            dma((halves, groups)),
            dma((halves, groups)),
            dma((halves, columns)),
            dma((halves, columns)),
        ],
        compiler_params=pltpu.CompilerParams(collective_id=0, has_side_effects=True),
    )(slot_subgrid, vis_count, offset, contributions, uv, obs, weight)


def grid_call(offsets, gathered, per_group, side, rows, gain):
    lanes = gathered.shape[-1]
    span = side + BLOCK
    width = 2 * per_group * rows
    return pl.pallas_call(
        functools.partial(grid_kernel, per_group, side, gain),
        out_shape=jax.ShapeDtypeStruct((per_group, 2, rows, WIN), jnp.float32),
        in_specs=[
            pl.BlockSpec(memory_space=pltpu.SMEM),
            pl.BlockSpec(memory_space=pltpu.VMEM),
        ],
        out_specs=pl.BlockSpec(memory_space=pltpu.VMEM),
        scratch_shapes=[
            pltpu.VMEM((WIN + side, width), jnp.float32),
            [pltpu.VMEM((width, 2 * lanes), jnp.bfloat16)] * 2,
            [pltpu.VMEM((span, 2 * lanes), jnp.bfloat16)] * 2,
            pltpu.SMEM((offsets.shape[0] * offsets.shape[1] + 8,), jnp.int32),
        ],
    )(offsets, gathered)


def body(contributions, slot_subgrid, vis_count, vis_uv, vis_obs, vis_weight, subgrid_offset):
    groups = lax.axis_size("facet")
    columns = lax.axis_size("sub")
    per_group, _, members, _, side, _ = contributions.shape
    lanes = vis_weight.shape[-1]
    gathered, offsets = exchange_call(
        groups,
        columns,
        slot_subgrid,
        vis_count,
        subgrid_offset,
        contributions,
        vis_uv,
        vis_obs,
        vis_weight,
    )
    gain = WIN / (side * math.sqrt(members * columns)) / math.sqrt(lanes)
    return grid_call(offsets, gathered, per_group, side, WIN // columns, gain)


def solution(mesh):
    placed = (
        P("facet", "sub", None, None, None, None),
        P("sub", None, None),
        P("facet", "sub", None),
        P("facet", "sub", None, None, None),
        P("facet", "sub", None, None, None),
        P("facet", "sub", None, None),
        P("sub", None, None),
    )
    return jax.shard_map(
        body, mesh=mesh, in_specs=placed, out_specs=P("facet", None, "sub", None), check_vma=False
    )
```
